32 devices in a mesh: prow: 8 (over y, x, core), pcol: 4 (over z).
Axes of the slice: x: 2, y: 2, z: 4, core: 2. Of those that a mesh axis runs over, the one named last changes fastest.
Arguments:
- matrix: float32 [8192, 8192], P('prow', 'pcol'), as said below
- pivots: int32 [2, 128], replicated, may hold values from 0 to 8191, as said below
Outputs:
- factored: float32 [8192, 8192], P('prow', 'pcol')
The draws below stay inside these ranges and needn't reach their ends.
Inputs may be any that keep to these rules, and one draw needn't show every extreme that they name: pivots[s, j] lies between s * 128 + j and 8191; with these interchanges no further pivoting is needed for the 2 panels. `matrix`: all entries are finite. After the given interchanges, the leading 2 * 128 rows and columns of A factor without further interchanges.
All inputs are finite; a program needn't handle non-finite values.
Results may differ from the reference program's by a relative error of at most 0.0003.
Values sent between devices are 32-bit elements; how exact they have to be, the bound alone decides.
No kernel may reach another device: no remote copies, remote signals or barrier semaphores. Data moves between devices by JAX's collectives and lax.ppermute only.
A program may use at most 128 MiB of HBM per device.

```python
import math
import jax
import jax.numpy as jnp
from jax import lax

NB = 128
STEPS = 2
ROW_BLOCKS = 8
COL_BLOCKS = 16
ORDER = 8192
N_PROW = 8
N_PCOL = 4


def pivot_table(key):
    sub_key = jax.random.fold_in(key, 7)
    lowest = jnp.arange(STEPS, dtype=jnp.int32)[:, None] * NB + jnp.arange(NB, dtype=jnp.int32)[None, :]
    table = jax.random.randint(sub_key, (STEPS, NB), lowest, ORDER, dtype=jnp.int32)
    top_slot = jax.random.randint(jax.random.fold_in(key, 9), (), 0, NB, dtype=jnp.int32)
    table = table.at[STEPS - 1, top_slot].set(ORDER - 1)
    return table.at[0, 0].set(0)


def draw_pivots(key, part):
    return pivot_table(key)


def draw_matrix(key, part):
    pivot_flat = pivot_table(key).reshape(-1)
    base_key = jax.random.fold_in(key, 11)
    keys = jax.random.split(base_key, 6)
    leading = STEPS * NB
    scaled = jax.random.truncated_normal(keys[0], -4.0, 4.0, (ORDER, ORDER), jnp.float32)
    spread = max(0.3, math.sqrt(4.5 / leading))
    lower_noise = jax.random.uniform(keys[2], (leading, leading), jnp.float32, -spread, spread)
    upper_noise = jax.random.uniform(keys[3], (leading, leading), jnp.float32, -spread, spread)
    magnitude = jax.random.uniform(keys[4], (leading,), jnp.float32, 1.0, 2.0)
    sign_flip = 1.0 - 2.0 * jax.random.randint(keys[5], (leading,), 0, 2).astype(jnp.float32)
    lead_ids = jnp.arange(leading, dtype=jnp.int32)
    same_place = lead_ids[:, None] == lead_ids[None, :]
    lower_factor = jnp.where(lead_ids[:, None] > lead_ids[None, :], lower_noise, same_place.astype(jnp.float32))
    diag_values = (magnitude * sign_flip)[:, None]
    upper_factor = jnp.where(lead_ids[:, None] < lead_ids[None, :], upper_noise, jnp.where(same_place, diag_values, 0.0))
    product = jnp.dot(lower_factor, upper_factor, precision=lax.Precision.HIGHEST, preferred_element_type=jnp.float32)
    square = math.sqrt(leading) * product
    prepared = scaled.at[:leading, :leading].set(square)

    def exchange_rows(j, labels):
        lower_pos = pivot_flat[j]
        first_label = labels[j]
        second_label = labels[lower_pos]
        return labels.at[j].set(second_label).at[lower_pos].set(first_label)
    labels = lax.fori_loop(0, leading, exchange_rows, jnp.arange(ORDER, dtype=jnp.int32))
    inverse = jnp.zeros((ORDER,), jnp.int32).at[labels].set(jnp.arange(ORDER, dtype=jnp.int32))
    natural = prepared[inverse]
    grid_rows = ORDER // (ROW_BLOCKS * NB)
    grid_cols = ORDER // (COL_BLOCKS * NB)
    shaped = natural.reshape(ROW_BLOCKS, grid_rows, NB, COL_BLOCKS, grid_cols, NB)
    return shaped.transpose(1, 0, 2, 4, 3, 5).reshape(ORDER, ORDER)


def setup_inputs(seed: int = 0) -> dict:
    key_of = jax.random.split(jax.random.key(seed), 3)
    matrix = draw_matrix(jax.random.fold_in(key_of[2], 71), 0)
    pivots = draw_pivots(jax.random.fold_in(key_of[2], 71), 0)
    return {"matrix": matrix, "pivots": pivots}


def matmul(left_side, right_side):
    return jnp.dot(left_side, right_side, precision=lax.Precision.HIGHEST, preferred_element_type=jnp.float32)


def swap_labels(pivot_list, first_row, full_order):
    def exchange_rows(j, labels):
        upper_pos = first_row + j
        lower_pos = pivot_list[j]
        first_label = labels[upper_pos]
        second_label = labels[lower_pos]
        return labels.at[upper_pos].set(second_label).at[lower_pos].set(first_label)

    return lax.fori_loop(0, pivot_list.shape[0], exchange_rows, jnp.arange(full_order, dtype=jnp.int32))


def lu_block(square):
    block_size = square.shape[0]
    positions = jnp.arange(block_size, dtype=jnp.int32)

    def eliminate(k, matrix_work):
        pivot_value = matrix_work[k, k]
        under_mask = positions > k
        column = jnp.where(under_mask, matrix_work[:, k] / pivot_value, 0.0)
        pivot_row = jnp.where(under_mask, matrix_work[k, :], 0.0)
        matrix_work = matrix_work - column[:, None] * pivot_row[None, :]
        return matrix_work.at[:, k].set(jnp.where(under_mask, column, matrix_work[:, k]))

    return lax.fori_loop(0, block_size, eliminate, square)


def tri_inverses(factors):
    block_size = factors.shape[0]
    positions = jnp.arange(block_size, dtype=jnp.int32)
    identity = (positions[:, None] == positions[None, :]).astype(factors.dtype)

    def forward(k, matrix_work):
        multiplier = jnp.where(positions > k, factors[:, k], 0.0)
        return matrix_work - multiplier[:, None] * matrix_work[k][None, :]

    def backward(j, matrix_work):
        k = block_size - 1 - j
        scaled_row = matrix_work[k] / factors[k, k]
        matrix_work = matrix_work.at[k].set(scaled_row)
        multiplier = jnp.where(positions < k, factors[:, k], 0.0)
        return matrix_work - multiplier[:, None] * scaled_row[None, :]

    lower_inv = lax.fori_loop(0, block_size, forward, identity)
    upper_inv = lax.fori_loop(0, block_size, backward, identity)
    return lower_inv, upper_inv


def to_natural(stored):
    shaped = stored.reshape(N_PROW, ROW_BLOCKS, NB, N_PCOL, COL_BLOCKS, NB)
    return shaped.transpose(1, 0, 2, 4, 3, 5).reshape(ORDER, ORDER)


def to_storage(natural):
    shaped = natural.reshape(ROW_BLOCKS, N_PROW, NB, COL_BLOCKS, N_PCOL, NB)
    return shaped.transpose(1, 0, 2, 4, 3, 5).reshape(ORDER, ORDER)


def reference(matrix, pivots):
    natural = to_natural(matrix)
    for s in range(STEPS):
        top_start = s * NB
        start_row = top_start + NB
        labels = swap_labels(pivots[s], top_start, ORDER)
        natural = natural[labels]
        factors = lu_block(natural[top_start:start_row, top_start:start_row])
        lower_inv, upper_inv = tri_inverses(factors)
        lower_part = matmul(natural[start_row:, top_start:start_row], upper_inv)
        upper_rows = matmul(lower_inv, natural[top_start:start_row, start_row:])
        natural = natural.at[start_row:, start_row:].add(-matmul(lower_part, upper_rows))
        natural = natural.at[start_row:, top_start:start_row].set(lower_part)
        natural = natural.at[top_start:start_row, top_start:start_row].set(factors)
        natural = natural.at[top_start:start_row, start_row:].set(upper_rows)
    return to_storage(natural)
```

```python
import functools

import jax
import jax.numpy as jnp
from jax import lax
from jax.experimental import pallas as pl
from jax.experimental.pallas import tpu as pltpu
from jax.sharding import PartitionSpec as P

NB = 128
TILE = 8
VMEM = pltpu.VMEM
SMEM = pltpu.SMEM
ANY = pl.ANY


def dot_full(left, right):
    return jnp.dot(left, right, precision=lax.Precision.HIGHEST, preferred_element_type=jnp.float32)


def split_bf16(value):
    high = value.astype(jnp.bfloat16)
    low = (value - high.astype(jnp.float32)).astype(jnp.bfloat16)
    return high, low


def dot_bf16(left, right):
    return jnp.dot(left, right, preferred_element_type=jnp.float32)


def pick_kernel(grid_rows, piv_ref, rank_ref, mat_ref, pick_ref, place_ref, root_ref, table_ref, sem):
    lead = piv_ref.shape[0]
    me = rank_ref[0]

    def prepare(j, carry):
        table_ref[piv_ref[j]] = piv_ref[j]
        return carry

    lax.fori_loop(0, lead, prepare, 0, unroll=8)

    def prepare_top(j, carry):
        table_ref[j] = j
        return carry

    lax.fori_loop(0, lead, prepare_top, 0, unroll=8)
    pick_ref[...] = jnp.zeros_like(pick_ref)

    def owned(row):
        block = row >> (NB.bit_length() - 1)
        if grid_rows & (grid_rows - 1) == 0:
            turn, rank = block >> (grid_rows.bit_length() - 1), block & (grid_rows - 1)
        else:
            turn, rank = lax.div(block, grid_rows), lax.rem(block, grid_rows)
        return rank == me, turn * NB + (row & (NB - 1))

    def copy_of(place, j):
        return pltpu.make_async_copy(mat_ref.at[pl.ds(place, 1)], pick_ref.at[pl.ds(j, 1)], sem)

    def exchange(j, count):
        other = piv_ref[j]
        upper = table_ref[j]
        lower = table_ref[other]
        table_ref[other] = upper
        table_ref[j] = lower
        mine, place = owned(lower)

        @pl.when(mine)
        def _():
            copy_of(place, j).start()

        return count + mine.astype(jnp.int32)

    count = lax.fori_loop(0, lead, exchange, 0)

    def leave(j, carry):
        other = piv_ref[j]
        mine, place = owned(other)
        place_ref[j] = jnp.where(mine & (other >= lead), place, -1)
        root_ref[j] = jnp.where(other >= lead, table_ref[other], 0)
        return carry

    lax.fori_loop(0, lead, leave, 0)

    def finish(j, carry):
        copy_of(0, 0).wait()
        return carry

    lax.fori_loop(0, count, finish, 0)


def pick_rows(matrix, pivots, row_rank, grid_rows):
    rows_dev, cols_dev = matrix.shape
    lead = pivots.shape[0] * pivots.shape[1]
    return pl.pallas_call(
        functools.partial(pick_kernel, grid_rows),
        out_shape=(
            jax.ShapeDtypeStruct((lead, cols_dev), jnp.float32),
            jax.ShapeDtypeStruct((lead,), jnp.int32),
            jax.ShapeDtypeStruct((lead,), jnp.int32),
        ),
        in_specs=[
            pl.BlockSpec(memory_space=SMEM),
            pl.BlockSpec(memory_space=SMEM),
            pl.BlockSpec(memory_space=ANY),
        ],
        out_specs=(
            pl.BlockSpec(memory_space=VMEM),
            pl.BlockSpec(memory_space=SMEM),
            pl.BlockSpec(memory_space=SMEM),
        ),
        scratch_shapes=[SMEM((rows_dev * grid_rows,), jnp.int32), pltpu.SemaphoreType.DMA],
        name="pick_rows",
    )(pivots.reshape(-1), row_rank.reshape(1), matrix)


def lu_tiles(square):
    size = square.shape[0]
    groups = size // TILE
    sub = lax.broadcasted_iota(jnp.int32, (TILE, size), 0)
    lane = lax.broadcasted_iota(jnp.int32, (TILE, size), 1)
    work = [square[g * TILE : (g + 1) * TILE] for g in range(groups)]
    left = [(lane == sub + g * TILE).astype(jnp.float32) for g in range(groups)]
    right = list(left)
    scale = jnp.zeros((TILE, size), jnp.float32)
    for k in range(size):
        own, i = k // TILE, k % TILE
        row = jnp.broadcast_to(work[own][i : i + 1], (TILE, size))
        row_left = jnp.broadcast_to(left[own][i : i + 1], (TILE, size))
        pivot = jnp.broadcast_to(row[:, k : k + 1], (TILE, size))
        inverse = 1.0 / pivot
        scale = jnp.where(lane == k, inverse, scale)
        row = jnp.where(lane > k, row, 0.0)
        row_scaled = row * inverse
        for g in range(own + 1):
            column = jnp.broadcast_to(right[g][:, k : k + 1], (TILE, size))
            right[g] = right[g] - column * row_scaled
        for g in range(own, groups):
            if g == own and i == TILE - 1:
                continue
            column = jnp.broadcast_to(work[g][:, k : k + 1], (TILE, size)) * inverse
            updated = work[g] - column * row
            if g == own:
                under = sub > i
                column = jnp.where(under, column, 0.0)
                updated = jnp.where(under, updated, work[g])
                work[g] = jnp.where((lane == k) & under, column, updated)
            else:
                work[g] = jnp.where(lane == k, column, updated)
            left[g] = left[g] - column * row_left
    right = [tile * scale for tile in right]
    return jnp.concatenate(work, 0), jnp.concatenate(left, 0), jnp.concatenate(right, 0)


def factor_kernel(block_ref, fac_ref, low_ref, up_ref):
    size = block_ref.shape[0]
    half = NB
    fac0, low0, up0 = lu_tiles(block_ref[:half, :half])
    upper = dot_full(low0, block_ref[:half, half:])
    lower = dot_full(block_ref[half:, :half], up0)
    schur = block_ref[half:, half:] - dot_full(lower, upper)
    fac1, low1, up1 = lu_tiles(schur)
    zeros = jnp.zeros((half, size - half), jnp.float32)
    fac_ref[:half, :half] = fac0
    fac_ref[:half, half:] = upper
    fac_ref[half:, :half] = lower
    fac_ref[half:, half:] = fac1
    low_ref[:half, :half] = low0
    low_ref[:half, half:] = zeros
    low_ref[half:, :half] = -dot_full(low1, dot_full(lower, low0))
    low_ref[half:, half:] = low1
    up_ref[:half, :half] = up0
    up_ref[:half, half:] = -dot_full(dot_full(up0, upper), up1)
    up_ref[half:, :half] = zeros
    up_ref[half:, half:] = up1


def factor(block):
    shape = jax.ShapeDtypeStruct(block.shape, jnp.float32)
    return pl.pallas_call(
        factor_kernel,
        out_shape=(shape, shape, shape),
        in_specs=[pl.BlockSpec(memory_space=VMEM)],
        out_specs=tuple(pl.BlockSpec(memory_space=VMEM) for _ in range(3)),
        name="factor",
    )(block)


def update_kernel(
    rank_ref, place_ref, root_ref, mat_ref, panel_ref, top_ref, old_ref, old_panel_ref, fac_ref, low_ref, up_ref,
    out_ref, work_ref, uf_ref, uh_ref, ul_ref, lp_ref, in_sem, out_sem,
):
    rows, cols = work_ref.shape
    lead = top_ref.shape[0]
    steps = lead // NB
    chunks = rows // NB
    row_rank, col_rank = rank_ref[0], rank_ref[1]

    def chunk(c):
        return pl.ds(c * NB, NB)

    def load(c):
        return pltpu.make_async_copy(mat_ref.at[chunk(c)], work_ref.at[chunk(c)], in_sem.at[c])

    def save(c):
        return pltpu.make_async_copy(work_ref.at[chunk(c)], out_ref.at[chunk(c)], out_sem.at[c])

    for c in range(chunks):
        load(c).start()
    upper = dot_full(low_ref[...], top_ref[...])
    uf_ref[...] = upper
    high, low = split_bf16(upper)
    uh_ref[...] = high
    ul_ref[...] = low
    lp_ref[...] = panel_ref[...]
    for c in range(chunks):
        load(c).wait()

    def place_row(j, carry):
        place = place_ref[j]

        @pl.when(place >= 0)
        def _():
            root = root_ref[j]
            lp_ref[pl.ds(place, 1), :] = old_panel_ref[pl.ds(root, 1), :]
            work_ref[pl.ds(place, 1), :] = old_ref[pl.ds(root, 1), :]

        return carry

    lax.fori_loop(0, lead, place_row, 0)
    for c in range(chunks):
        part = dot_full(lp_ref[c * NB : (c + 1) * NB], up_ref[...])
        lp_ref[c * NB : (c + 1) * NB] = part
        high, low = split_bf16(part)
        delta = dot_bf16(high, uh_ref[...]) + (dot_bf16(high, ul_ref[...]) + dot_bf16(low, uh_ref[...]))
        work_ref[c * NB : (c + 1) * NB] = work_ref[c * NB : (c + 1) * NB] - delta
        for s in range(steps):

            @pl.when(col_rank == s)
            def _():
                work_ref[c * NB : (c + 1) * NB, :NB] = lp_ref[c * NB : (c + 1) * NB, s * NB : (s + 1) * NB]

        if c == 0:
            for s in range(steps):

                @pl.when(row_rank == s)
                def _():
                    work_ref[:NB] = uf_ref[s * NB : (s + 1) * NB]
                    for q in range(steps):

                        @pl.when(col_rank == q)
                        def _():
                            work_ref[:NB, :NB] = fac_ref[s * NB : (s + 1) * NB, q * NB : (q + 1) * NB]

        save(c).start()
    for c in range(chunks):
        save(c).wait()


def update(ranks, place, root, matrix, panel, top, old, old_panel, fac, low, up):
    rows, cols = matrix.shape
    lead = top.shape[0]
    chunks = rows // NB
    in_vmem = pl.BlockSpec(memory_space=VMEM)
    in_smem = pl.BlockSpec(memory_space=SMEM)
    anywhere = pl.BlockSpec(memory_space=ANY)
    return pl.pallas_call(
        update_kernel,
        out_shape=jax.ShapeDtypeStruct(matrix.shape, jnp.float32),
        in_specs=[in_smem] * 3 + [anywhere] + [in_vmem] * 7,
        out_specs=anywhere,
        scratch_shapes=[
            VMEM((rows, cols), jnp.float32),
            VMEM((lead, cols), jnp.float32),
            VMEM((lead, cols), jnp.bfloat16),
            VMEM((lead, cols), jnp.bfloat16),
            VMEM((rows, lead), jnp.float32),
            pltpu.SemaphoreType.DMA((chunks,)),
            pltpu.SemaphoreType.DMA((chunks,)),
        ],
        name="update",
    )(ranks, place, root, matrix, panel, top, old, old_panel, fac, low, up)


def swap_bit(value, axis, bit):
    size = lax.axis_size(axis)
    return lax.ppermute(value, axis, [(i, i ^ bit) for i in range(size)])


def reduce_half(value, axis, bit):
    half = value.shape[0] // 2
    upper = (lax.axis_index(axis) // bit) % 2 == 1
    keep = jnp.where(upper, value[half:], value[:half])
    give = jnp.where(upper, value[:half], value[half:])
    return keep + swap_bit(give, axis, bit)


def gather_half(value, axis, bit, dim=0):
    upper = (lax.axis_index(axis) // bit) % 2 == 1
    other = swap_bit(value, axis, bit)
    return jnp.concatenate([jnp.where(upper, other, value), jnp.where(upper, value, other)], axis=dim)


def tree(value, axis, bit, first):
    size = lax.axis_size(axis)
    pairs = [(i, i + bit) for i in range(size) if i % (2 * bit) < first and i % (2 * bit) < bit]
    got = lax.ppermute(value, axis, pairs)
    mine = lax.axis_index(axis) % (2 * bit) < first
    return jnp.where(mine, value, got)


def local(matrix, pivots):
    steps = pivots.shape[0]
    grid_rows = lax.axis_size("prow")
    grid_cols = lax.axis_size("pcol")
    row_rank = lax.axis_index("prow")
    col_rank = lax.axis_index("pcol")
    row_bits = [1 << b for b in range(1, grid_rows.bit_length() - 1)]
    col_bits = [1 << b for b in range(1, grid_cols.bit_length() - 1)]
    ranks = jnp.stack([row_rank, col_rank]).astype(jnp.int32)

    panel = matrix[:, :NB]
    for bit in reversed(col_bits):
        panel = tree(panel, "pcol", bit, steps)
    panel = gather_half(panel, "pcol", 1, 1)

    old = matrix[:NB]
    old_panel = matrix[:NB, :NB]
    for bit in reversed(row_bits):
        old_panel = tree(old_panel, "prow", bit, steps)
        old = tree(old, "prow", bit, steps)

    picked, place, root = pick_rows(matrix, pivots, row_rank.astype(jnp.int32), grid_rows)
    block = reduce_half(picked[:, :NB], "prow", 1)
    for bit in row_bits:
        block = block + swap_bit(block, "prow", bit)
    block = jnp.concatenate([block, old_panel], axis=0)
    for bit in reversed(col_bits):
        block = tree(block, "pcol", bit, steps)
    block = gather_half(block, "pcol", 1, 1)
    block = gather_half(block[None], "prow", 1)
    old_panel = block[:, NB:].reshape(steps * NB, steps * NB)
    block = block[:, :NB].reshape(steps * NB, steps * NB)
    fac, low, up = factor(block)

    top = picked
    for bit in [1] + row_bits:
        top = reduce_half(top, "prow", bit)
    for bit in reversed(row_bits):
        top = gather_half(top, "prow", bit)
    both = gather_half(jnp.stack([top, old])[None], "prow", 1)
    top = both[:, 0].reshape(steps * NB, -1)
    old = both[:, 1].reshape(steps * NB, -1)
    return update(ranks, place, root, matrix, panel, top, old, old_panel, fac, low, up)


def solution(mesh):
    return jax.shard_map(
        local,
        mesh=mesh,
        in_specs=(P("prow", "pcol"), P()),
        out_specs=P("prow", "pcol"),
        check_vma=False,
    )
```

```python
import functools

import jax
import jax.numpy as jnp
from jax import lax
from jax.experimental import pallas as pl
from jax.experimental.pallas import tpu as pltpu
from jax.sharding import PartitionSpec as P


NB = 128
TILE = 8
VMEM = pltpu.VMEM
SMEM = pltpu.SMEM
ANY = pl.ANY


def dot_full(left, right):
    return jnp.dot(left, right, precision=lax.Precision.HIGHEST, preferred_element_type=jnp.float32)


def split_bf16(value):
    high = value.astype(jnp.bfloat16)
    low = (value - high.astype(jnp.float32)).astype(jnp.bfloat16)
    return high, low


def dot_bf16(left, right):
    return jnp.dot(left, right, preferred_element_type=jnp.float32)


def wide_left(value):
    high, low = split_bf16(value)
    return jnp.concatenate([high, high, low], axis=1)


def wide_right(value):
    high, low = split_bf16(value)
    return jnp.concatenate([high, low, high], axis=0)


def reversed_bits(value, size):
    count = size.bit_length() - 1
    return sum(((value >> b) & 1) << (count - 1 - b) for b in range(count))


def split_exact(value):
    high = value.astype(jnp.bfloat16)
    rest = value - high.astype(jnp.float32)
    middle = rest.astype(jnp.bfloat16)
    return high, middle, (rest - middle.astype(jnp.float32)).astype(jnp.bfloat16)


def select_rows(chosen, value):
    high, middle, low = split_exact(value)
    return (dot_bf16(chosen, high) + dot_bf16(chosen, middle)) + dot_bf16(chosen, low)


def plan_kernel(
    grid_rows, row_ref, piv_ref, mat_ref, keep_ref, give_ref, table_ref, panel_ref, small_ref, first_ref, second_ref, link_ref, sems
):
    lead = piv_ref.shape[1]
    rows = panel_ref.shape[0]
    part = first_ref.shape[1]
    me = row_ref[0]
    load = pltpu.make_async_copy(mat_ref.at[:, pl.ds(0, NB)], panel_ref, sems.at[0])
    load_first = pltpu.make_async_copy(mat_ref.at[pl.ds(0, NB), pl.ds(0, part)], first_ref, sems.at[1])
    load_second = pltpu.make_async_copy(mat_ref.at[pl.ds(0, NB), pl.ds(part, part)], second_ref, sems.at[2])
    load.start()
    load_first.start()
    load_second.start()
    row_id = lax.broadcasted_iota(jnp.int32, (lead, lead), 0).astype(jnp.float32)
    col_id = lax.broadcasted_iota(jnp.int32, (lead, lead), 1).astype(jnp.float32)
    pivots = piv_ref[...]
    along = jnp.broadcast_to(pivots.astype(jnp.float32), (lead, lead))
    own = jnp.sum(jnp.where(row_id == col_id, along, 0.0), axis=1, keepdims=True)
    earlier = col_id < row_id
    parent = jnp.max(jnp.where((along == row_id) & earlier, col_id, -1.0), axis=1, keepdims=True)
    parent = jnp.where(parent < 0.0, row_id[:, :1], parent)
    prior = jnp.max(jnp.where((along == own) & earlier, col_id, -1.0), axis=1, keepdims=True)
    link_ref[...] = jnp.where(col_id == parent, 1.0, 0.0)

    def jump(changed):
        old = link_ref[...]
        link = old.astype(jnp.bfloat16)
        new = dot_bf16(link, link)
        link_ref[...] = new
        return jnp.max(jnp.abs(new - old)) > 0.0

    lax.while_loop(lambda changed: changed, jump, True)
    link = link_ref[...].astype(jnp.bfloat16)
    previous = jnp.where(col_id == prior, 1.0, 0.0).astype(jnp.bfloat16)
    origin = jnp.sum(dot_bf16(previous, link) * col_id, axis=1, keepdims=True)
    source = jnp.where(prior < 0.0, own, origin)
    shift = NB.bit_length() - 1

    def owner_of(block):
        if grid_rows & (grid_rows - 1) == 0:
            return block & (grid_rows - 1), block >> (grid_rows.bit_length() - 1)
        return lax.rem(block, grid_rows), lax.div(block, grid_rows)

    held = lax.broadcasted_iota(jnp.int32, (1, rows), 1)
    held = (((held >> shift) * grid_rows + me) * NB + (held & (NB - 1))).astype(jnp.float32)
    chosen = jnp.where(source == held, 1.0, 0.0).astype(jnp.bfloat16)
    load.wait()
    small_ref[...] = panel_ref[:NB]
    picked = select_rows(chosen, panel_ref[...])
    half = lead // 2
    keep_ref[...] = jnp.where((me & 1) == 0, picked[:half], picked[half:])
    give_ref[...] = jnp.where((me & 1) == 0, picked[half:], picked[:half])

    def along_lanes(table):
        ids = col_id[:TILE].astype(jnp.bfloat16)
        return lax.dot_general(ids, table, (((1,), (1,)), ((), ())), preferred_element_type=jnp.float32)[:1]

    def local_row(row, valid):
        rank, turn = owner_of(row >> shift)
        return jnp.where((rank == me) & valid, turn * NB + (row & (NB - 1)), -1)

    alike = along.T == along
    reused = jnp.max(jnp.where(alike & (row_id < col_id), 1.0, 0.0), axis=0, keepdims=True) > 0.0
    final = jnp.max(jnp.where(alike & (row_id > col_id), 1.0, 0.0), axis=0, keepdims=True) < 1.0
    origin_along = along_lanes(dot_bf16(previous, link).astype(jnp.bfloat16)).astype(jnp.int32)
    leaving = local_row(pivots, (pivots >= lead) & final)
    entering = local_row(jnp.where(reused, origin_along, pivots), jnp.full(pivots.shape, True))
    roots = along_lanes(link)
    upto = jnp.where(row_id <= col_id, 1.0, 0.0).astype(jnp.bfloat16)
    near = jnp.where(roots >= NB, 1, 0) == (me & 1)
    masks = [(leaving >= 0) & near, (leaving >= 0) & ~near, entering >= 0]
    spare = jnp.zeros((TILE - len(masks), lead), jnp.float32)
    ones = [jnp.where(mask, 1.0, 0.0) for mask in masks]
    counts = dot_bf16(jnp.concatenate(ones + [spare], axis=0).astype(jnp.bfloat16), upto)
    for n, (value, other) in enumerate(((leaving, roots), (leaving, roots), (entering, col_id[:1]))):
        spot = (row_id == counts[n : n + 1] - 1.0) & masks[n]
        high, low = (value >> shift).astype(jnp.float32), (value & (NB - 1)).astype(jnp.float32)
        entries = jnp.concatenate([high, low, other, jnp.zeros((TILE - 3, lead), jnp.float32)], axis=0)
        spot = jnp.where(spot, 1.0, 0.0).astype(jnp.bfloat16)
        packed = lax.dot_general(
            entries.astype(jnp.bfloat16), spot, (((1,), (1,)), ((), ())), preferred_element_type=jnp.float32
        ).astype(jnp.int32)
        table_ref[3 * n : 3 * n + 1] = packed[0:1] * NB + packed[1:2]
        table_ref[3 * n + 1 : 3 * n + 2] = packed[2:3]
        table_ref[3 * n + 2 : 3 * n + 3] = counts[n : n + 1].astype(jnp.int32)
    load_first.wait()
    load_second.wait()


def plan_rows(matrix, pivots, ranks, grid_rows):
    rows, cols = matrix.shape
    lead = pivots.size
    half = jax.ShapeDtypeStruct((lead // 2, NB), jnp.float32)
    part = jax.ShapeDtypeStruct((NB, cols // 2), jnp.float32)
    return pl.pallas_call(
        functools.partial(plan_kernel, grid_rows),
        out_shape=(
            half,
            half,
            jax.ShapeDtypeStruct((9, lead), jnp.int32),
            jax.ShapeDtypeStruct((rows, NB), jnp.float32),
            jax.ShapeDtypeStruct((NB, NB), jnp.float32),
            part,
            part,
        ),
        in_specs=[
            pl.BlockSpec(memory_space=SMEM),
            pl.BlockSpec(memory_space=VMEM),
            pl.BlockSpec(memory_space=ANY),
        ],
        out_specs=tuple(pl.BlockSpec(memory_space=VMEM) for _ in range(7)),
        scratch_shapes=[VMEM((lead, lead), jnp.float32), pltpu.SemaphoreType.DMA((3,))],
        name="plan_rows",
    )(ranks[0], pivots.reshape(1, lead), matrix)


def pick_kernel(grid_rows, row_ref, table_ref, mat_ref, keep_ref, give_ref, sem):
    half = keep_ref.shape[0]
    unit = 2 * half // grid_rows
    shift = unit.bit_length() - 1
    order = reversed_bits(row_ref[0], grid_rows)
    count = table_ref[8, 2 * half - 1]
    keep_ref[...] = jnp.zeros_like(keep_ref)
    give_ref[...] = jnp.zeros_like(give_ref)

    def copy_of(place, ref, spot):
        return pltpu.make_async_copy(mat_ref.at[pl.ds(place, 1)], ref.at[pl.ds(spot, 1)], sem)

    def pick(r, carry):
        place, slot = table_ref[6, r], table_ref[7, r]
        spot = (((slot >> shift) ^ order) << shift) | (slot & (unit - 1))

        @pl.when(spot < half)
        def _():
            copy_of(place, keep_ref, spot).start()

        @pl.when(spot >= half)
        def _():
            copy_of(place, give_ref, spot - half).start()

        return carry

    lax.fori_loop(0, count, pick, 0)

    def finish(r, carry):
        copy_of(0, keep_ref, 0).wait()
        return carry

    lax.fori_loop(0, count, finish, 0)


def pick_rows(matrix, table, ranks, grid_rows):
    cols = matrix.shape[1]
    half = jax.ShapeDtypeStruct((table.shape[1] // 2, cols), jnp.float32)
    return pl.pallas_call(
        functools.partial(pick_kernel, grid_rows),
        out_shape=(half, half),
        in_specs=[
            pl.BlockSpec(memory_space=SMEM),
            pl.BlockSpec(memory_space=SMEM),
            pl.BlockSpec(memory_space=ANY),
        ],
        out_specs=(pl.BlockSpec(memory_space=VMEM), pl.BlockSpec(memory_space=VMEM)),
        scratch_shapes=[pltpu.SemaphoreType.DMA],
        name="pick_rows",
    )(ranks[0], table, matrix)


def lu_tiles(square):
    size = square.shape[0]
    groups = size // TILE
    sub = lax.broadcasted_iota(jnp.int32, (TILE, size), 0)
    lane = lax.broadcasted_iota(jnp.int32, (TILE, size), 1)

    def across(tile, k):
        return jnp.broadcast_to(tile[:, k : k + 1], (TILE, size))

    def down(tile, i):
        return jnp.broadcast_to(tile[i : i + 1], (TILE, size))

    work = [square[g * TILE : (g + 1) * TILE] for g in range(groups)]
    left = [(lane == sub + g * TILE).astype(jnp.float32) for g in range(groups)]
    right = list(left)
    for g in range(groups):
        base = g * TILE
        cols = {r: [across(work[r], base + j) for j in range(TILE)] for r in (g, g + 1) if r < groups}
        own, own_left = work[g], left[g]
        inverses, rows, rows_left, uppers = [], [], [], {}
        for i in range(TILE):
            inverse = 1.0 / down(cols[g][i], i)
            inverses.append(inverse)
            for j in range(i + 1, TILE):
                uppers[i, j] = down(cols[g][j], i)
            rows.append(down(own, i))
            rows_left.append(down(own_left, i))
            factor_i = jnp.where(sub > i, cols[g][i] * inverse, 0.0)
            for j in range(i + 1, TILE):
                cols[g][j] = cols[g][j] - factor_i * uppers[i, j]
            own = own - factor_i * rows[i]
            own_left = own_left - factor_i * rows_left[i]
            cols[g][i] = jnp.where(sub > i, factor_i, cols[g][i])
            if g + 1 < groups:
                cols[g + 1][i] = cols[g + 1][i] * inverse
                for j in range(i + 1, TILE):
                    cols[g + 1][j] = cols[g + 1][j] - cols[g + 1][i] * uppers[i, j]
        own = jnp.where(lane >= base + TILE, own, work[g])
        for j in range(TILE):
            own = jnp.where(lane == base + j, cols[g][j], own)
        work[g], left[g] = own, own_left

        def marked(row, i, mark):
            return jnp.where(lane == base + i, mark, jnp.where(lane >= base + TILE, row, 0.0))

        narrow = [marked(rows[i], i, -1.0) for i in range(TILE)]
        if g + 1 < groups:
            r = g + 1
            tile = jnp.where((lane >= base) & (lane < base + TILE), 0.0, work[r])
            for i in range(TILE):
                tile = tile - cols[r][i] * narrow[i]
                left[r] = left[r] - cols[r][i] * rows_left[i]
            work[r] = tile
        scaled = {key: value * inverses[key[0]] for key, value in uppers.items()}
        backs = [marked(rows[i] * inverses[i], i, -inverses[i]) for i in range(TILE)]
        clear = (lane >= base) & (lane < base + TILE)
        lower = {r: [across(work[r], base + j) for j in range(TILE)] for r in range(g + 2, groups)}
        for r, parts in lower.items():
            tile = jnp.where(clear, 0.0, work[r])
            for i in range(TILE):
                parts[i] = parts[i] * inverses[i]
                for j in range(i + 1, TILE):
                    parts[j] = parts[j] - parts[i] * uppers[i, j]
                tile = tile - parts[i] * narrow[i]
                left[r] = left[r] - parts[i] * rows_left[i]
            work[r] = tile
        upper = {r: [across(right[r], base + j) for j in range(TILE)] for r in range(g + 1)}
        for r, parts in upper.items():
            tile = jnp.where(clear, 0.0, right[r])
            for i in range(TILE):
                for j in range(i + 1, TILE):
                    parts[j] = parts[j] - parts[i] * scaled[i, j]
                tile = tile - parts[i] * backs[i]
            right[r] = tile
    return jnp.concatenate(work, 0), jnp.concatenate(left, 0), jnp.concatenate(right, 0)


def factor_kernel(
    row_ref, col_ref, mine_same, mine_other, far_same, far_other, fac_ref, low_ref, up_ref, old_ref, block_ref
):
    size = block_ref.shape[0]
    half = NB
    for core in range(2):
        for col in range(2):

            @pl.when(((row_ref[0] & 1) == core) & ((col_ref[0] & 1) == col))
            def _():
                near, far = pl.ds(core * half, half), pl.ds((1 - core) * half, half)
                same, other = pl.ds(col * half, half), pl.ds((1 - col) * half, half)
                block_ref[near, same] = mine_same[:half]
                block_ref[near, other] = mine_other[:half]
                block_ref[far, same] = far_same[:half]
                block_ref[far, other] = far_other[:half]
                old_ref[near, same] = mine_same[half:]
                old_ref[near, other] = mine_other[half:]
                old_ref[far, same] = far_same[half:]
                old_ref[far, other] = far_other[half:]

    fac0, low0, up0 = lu_tiles(block_ref[:half, :half])
    upper = dot_full(low0, block_ref[:half, half:])
    lower = dot_full(block_ref[half:, :half], up0)
    schur = block_ref[half:, half:] - dot_full(lower, upper)
    fac1, low1, up1 = lu_tiles(schur)
    zeros = jnp.zeros((half, size - half), jnp.float32)
    fac_ref[:half, :half] = fac0
    fac_ref[:half, half:] = upper
    fac_ref[half:, :half] = lower
    fac_ref[half:, half:] = fac1
    low_ref[:half, :half] = low0
    low_ref[:half, half:] = zeros
    low_ref[half:, :half] = -dot_full(low1, dot_full(lower, low0))
    low_ref[half:, half:] = low1
    up_ref[:half, :half] = up0
    up_ref[:half, half:] = -dot_full(dot_full(up0, upper), up1)
    up_ref[half:, :half] = zeros
    up_ref[half:, half:] = up1


def factor(ranks, mine_same, mine_other, far_same, far_other):
    size = 2 * NB
    shape = jax.ShapeDtypeStruct((size, size), jnp.float32)
    return pl.pallas_call(
        factor_kernel,
        out_shape=(shape,) * 4,
        in_specs=[pl.BlockSpec(memory_space=SMEM)] * 2 + [pl.BlockSpec(memory_space=VMEM)] * 4,
        out_specs=tuple(pl.BlockSpec(memory_space=VMEM) for _ in range(4)),
        scratch_shapes=[VMEM((size, size), jnp.float32)],
        name="factor",
    )(*ranks, mine_same, mine_other, far_same, far_other)


def update_kernel(pieces, row_ref, col_ref, list_ref, mat_ref, panel_same, panel_other, *refs):
    top_refs, refs = refs[:pieces], refs[pieces:]
    old_near, old_far, refs = refs[0], refs[1], refs[2:]
    old_panel_ref, fac_ref, low_ref, up_ref, out_ref = refs[:5]
    work_ref, raw_ref, top_ref, lp_ref, wide_ref, in_sem, out_sem, top_sem, row_sem = refs[5:]
    _, cols = work_ref.shape
    lead = up_ref.shape[0]
    steps = lead // NB
    width = 4 * NB
    chunks = cols // width
    unit = lead // pieces
    row_rank, col_rank = row_ref[0], col_ref[0]
    order, col_turn = reversed_bits(row_rank, pieces), col_rank & 1
    lists = ((0, list_ref[2, lead - 1]), (3, list_ref[5, lead - 1]))
    count = lists[0][1] + lists[1][1]

    def chunk(c):
        return pl.ds(c * width, width)

    def load(c):
        return pltpu.make_async_copy(mat_ref.at[:, chunk(c)], work_ref.at[:, chunk(c)], in_sem.at[c])

    def save(c):
        return pltpu.make_async_copy(work_ref.at[:, chunk(c)], out_ref.at[:, chunk(c)], out_sem.at[c])

    def load_panel(n, ref, turn):
        to = lp_ref.at[:, pl.ds(pl.multiple_of(turn * NB, NB), NB)]
        return pltpu.make_async_copy(ref, to, in_sem.at[chunks + n])

    def load_top(u):
        to = raw_ref.at[pl.ds(pl.multiple_of((u ^ order) * unit, unit), unit)]
        return pltpu.make_async_copy(top_refs[u], to, top_sem.at[u])

    panels = [load_panel(0, panel_same, col_turn), load_panel(1, panel_other, 1 - col_turn)]
    for copy in panels:
        copy.start()
    for u in range(pieces):
        load_top(u).start()
    for c in range(chunks):
        load(c).start()
    for copy in panels:
        copy.wait()

    def panel_row(place, root):
        return pltpu.make_async_copy(old_panel_ref.at[pl.ds(root, 1)], lp_ref.at[pl.ds(place, 1)], row_sem)

    for first, length in lists:

        def place_panel(j, carry, first=first):
            panel_row(list_ref[first, j], list_ref[first + 1, j]).start()
            return carry

        lax.fori_loop(0, length, place_panel, 0)
    for u in range(pieces):
        load_top(u).wait()
    high, low = split_bf16(raw_ref[...])
    top_ref[:lead] = high
    top_ref[lead : 2 * lead] = low
    top_ref[2 * lead :] = high

    def wait_panel(j, carry):
        panel_row(0, 0).wait()
        return carry

    lax.fori_loop(0, count, wait_panel, 0)
    lower = dot_bf16(wide_left(lp_ref[...]), wide_right(up_ref[...]))
    lp_ref[...] = lower
    wide_ref[...] = wide_left(lower)
    for c in range(chunks):
        load(c).wait()

    def row_copy(ref, root, place):
        return pltpu.make_async_copy(ref.at[pl.ds(root & (NB - 1), 1)], work_ref.at[pl.ds(place, 1)], row_sem)

    for (first, length), old_ref in zip(lists, (old_near, old_far)):

        def place_row(j, carry, first=first, old_ref=old_ref):
            row_copy(old_ref, list_ref[first + 1, j], list_ref[first, j]).start()
            return carry

        lax.fori_loop(0, length, place_row, 0)
    wide_low = wide_left(low_ref[...])

    def upper_of(c):
        return dot_bf16(wide_low, top_ref[:, c * width : (c + 1) * width])

    def wait_row(j, carry):
        row_copy(old_near, 0, 0).wait()
        return carry

    upper = upper_of(0)
    for c in range(chunks):
        at = slice(c * width, (c + 1) * width)
        following = upper_of(c + 1) if c + 1 < chunks else None
        delta = dot_bf16(wide_ref[...], wide_right(upper))
        if c == 0:
            lax.fori_loop(0, count, wait_row, 0)
        value = work_ref[:, at] - delta
        head = value[:NB]
        for s in range(steps):
            head = jnp.where(row_rank == s, upper[s * NB : (s + 1) * NB], head)
        if c == 0:
            below, lower = value[NB:, :NB], lp_ref[...]
            lead_head = head[:, :NB]
            for q in range(steps):
                column = lower[:NB, q * NB : (q + 1) * NB]
                for s in range(steps):
                    column = jnp.where(row_rank == s, fac_ref[s * NB : (s + 1) * NB, q * NB : (q + 1) * NB], column)
                lead_head = jnp.where(col_rank == q, column, lead_head)
                below = jnp.where(col_rank == q, lower[NB:, q * NB : (q + 1) * NB], below)
            work_ref[:NB, :NB] = lead_head
            work_ref[:NB, NB:width] = head[:, NB:]
            work_ref[NB:, :NB] = below
            work_ref[NB:, NB:width] = value[NB:, NB:]
        else:
            work_ref[:NB, at] = head
            work_ref[NB:, at] = value[NB:]
        save(c).start()
        upper = following
    for c in range(chunks):
        save(c).wait()


def update(ranks, table, matrix, panels, tops, olds, old_panel, fac, low, up):
    rows, cols = matrix.shape
    lead = low.shape[0]
    chunks = cols // (4 * NB)
    in_vmem = pl.BlockSpec(memory_space=VMEM)
    in_smem = pl.BlockSpec(memory_space=SMEM)
    anywhere = pl.BlockSpec(memory_space=ANY)
    moved = list(panels) + list(tops) + list(olds) + [old_panel]
    values = moved + [fac, low, up]
    return pl.pallas_call(
        functools.partial(update_kernel, len(tops)),
        out_shape=jax.ShapeDtypeStruct(matrix.shape, jnp.float32),
        in_specs=[in_smem] * 3 + [anywhere] * (1 + len(moved)) + [in_vmem] * 3,
        out_specs=anywhere,
        scratch_shapes=[
            VMEM((rows, cols), jnp.float32),
            VMEM((lead, cols), jnp.float32),
            VMEM((3 * lead, cols), jnp.bfloat16),
            VMEM((rows, lead), jnp.float32),
            VMEM((rows, 3 * lead), jnp.bfloat16),
            pltpu.SemaphoreType.DMA((chunks + 2,)),
            pltpu.SemaphoreType.DMA((chunks,)),
            pltpu.SemaphoreType.DMA((len(tops),)),
            pltpu.SemaphoreType.DMA,
        ],
        name="update",
    )(*ranks, table, matrix, *values)


def swap_with(value, axis, mask):
    size = lax.axis_size(axis)
    return lax.ppermute(value, axis, [(i, i ^ mask) for i in range(size)])


def tree(value, axis, bit, bits_done, first):
    size = lax.axis_size(axis)
    reach = sum(bits_done)
    low = size - 1 - reach - bit
    holders = [i for i in range(size) if i & low & ~(first - 1) == 0 and i & bit == 0]
    got = lax.ppermute(value, axis, [(i, i + bit) for i in holders])
    return jnp.where(lax.axis_index(axis) & bit == 0, value, got)


def spread(value, axis, bits, first):
    done = []
    for bit in bits:
        value = tree(value, axis, bit, done, first)
        done.append(bit)
    return value


def local(matrix, pivots):
    lead = pivots.size
    steps = pivots.shape[0]
    grid_rows = lax.axis_size("prow")
    grid_cols = lax.axis_size("pcol")
    row_rank = lax.axis_index("prow")
    col_rank = lax.axis_index("pcol")
    row_bits = [1 << b for b in range(1, grid_rows.bit_length() - 1)]
    col_bits = [1 << b for b in range(1, grid_cols.bit_length() - 1)]
    ranks = (row_rank.astype(jnp.int32).reshape(1), col_rank.astype(jnp.int32).reshape(1))

    keep, give, table, panel, small, first, second = plan_rows(matrix, pivots, ranks, grid_rows)

    panel_near = spread(panel, "pcol", col_bits[::-1], steps)
    panels = (panel_near, swap_with(panel_near, "pcol", 1))
    old = jnp.concatenate(
        [spread(first, "prow", row_bits, steps), spread(second, "prow", row_bits[::-1], steps)], axis=1
    )
    olds = [old, swap_with(old, "prow", 1)]

    block = jnp.concatenate([keep + swap_with(give, "prow", 1), small], axis=0)
    for bit in row_bits:
        got = swap_with(block, "prow", bit)
        old_panel = jnp.where(row_rank & bit == 0, block[NB:], got[NB:])
        block = jnp.concatenate([block[:NB] + got[:NB], old_panel], axis=0)
    same = spread(block, "pcol", col_bits[::-1], steps)
    far_same = swap_with(same, "prow", 1)
    other = swap_with(same, "pcol", 1)
    far_other = swap_with(other, "prow", 1)
    fac, low, up, old_block = factor(ranks, same, other, far_same, far_other)

    keep, give = pick_rows(matrix, table, ranks, grid_rows)
    got = swap_with(give, "prow", 1)
    unit = lead // grid_rows
    masks = [2 * m for m in range(1, grid_rows // 2)]
    spots = [reversed_bits(mask, grid_rows) * unit for mask in masks]
    sums = [keep[spot : spot + unit] + got[spot : spot + unit] for spot in [0] + spots]
    total = sums[0]
    parts = [swap_with(value, "prow", mask) for mask, value in zip(masks, sums[1:])]
    for value in parts:
        total = total + value
    near = {0: total}
    for mask, spot in zip(masks, spots):
        near[spot] = swap_with(total, "prow", mask)
    near = [near[spot] for spot in sorted(near)]
    tops = near + [swap_with(piece, "prow", 1) for piece in near]
    return update(ranks, table, matrix, panels, tops, olds, old_block, fac, low, up)


def solution(mesh):
    return jax.shard_map(
        local,
        mesh=mesh,
        in_specs=(P("prow", "pcol"), P()),
        out_specs=P("prow", "pcol"),
        check_vma=False,
    )
```
